512 devices in a mesh: ctx: 256 (over z, y, x), hid: 2 (over core).
Axes of the slice: x: 4, y: 8, z: 8, core: 2. Of those that a mesh axis runs over, the one named last changes fastest.
Arguments:
- queries: bfloat16 [65536, 4096], P('ctx', 'hid'), may hold values from -8 to 8
- keys: bfloat16 [65536, 1024], P('ctx', 'hid'), may hold values from -5 to 5
- values: bfloat16 [65536, 1024], P('ctx', 'hid'), may hold values from -6 to 6
- residual: bfloat16 [65536, 4096], P('ctx', 'hid'), may hold values from -6 to 6
- out_weight: bfloat16 [4096, 4096], P('hid'), may hold values from -0.125 to 0.125
Outputs:
- layer_out: bfloat16 [65536, 4096], P('ctx', 'hid')
The draws below stay inside these ranges and needn't reach their ends.
All inputs are finite; a program needn't handle non-finite values.
Results may differ from the reference program's by a relative error of at most 0.0044.
Values may be sent and summed in bfloat16 or wider, within the bound.
No kernel may reach another device: no remote copies, remote signals or barrier semaphores. Data moves between devices by JAX's collectives and lax.ppermute only.
A program may use at most 64 MiB of HBM per device.

```python
import math
import jax
import jax.numpy as jnp
from jax import lax

D = 4096
QUERY_HEADS = 32
KEY_VALUE_HEADS = 8
HEAD_SIZE = 128
TOK_DEV = 256
SEQUENCE_LENGTH = 65536
N_CTX = 256


def joint_draw(key):
    base = jax.random.fold_in(key, 7)
    query_key, key_sampler = jax.random.split(base)
    queries = jnp.clip(jax.random.normal(query_key, (SEQUENCE_LENGTH, QUERY_HEADS * HEAD_SIZE), jnp.float32), -5.0, 5.0)
    keys = jnp.clip(jax.random.normal(key_sampler, (SEQUENCE_LENGTH, KEY_VALUE_HEADS * HEAD_SIZE), jnp.float32), -5.0, 5.0)
    return (queries, keys)


def draw_queries(key, part):
    return joint_draw(key)[0].astype(jnp.bfloat16)


def draw_keys(key, part):
    return joint_draw(key)[1].astype(jnp.bfloat16)


def spiked(drawn, stream_key, source, target, blocks, factor):
    def block_of(dim):
        return (jnp.arange(drawn.shape[dim]) // (drawn.shape[dim] // blocks)).reshape((-1,) + (1,) * (drawn.ndim - 1 - dim))

    first = jax.random.permutation(stream_key, blocks)[block_of(target)]
    far = (block_of(target) + blocks // 2) % blocks
    return jnp.where((block_of(source) == first) | (block_of(source) == far), factor * drawn, drawn)


def shard_levels(own_key, extent, pieces, low, largest):
    level = 1.0
    for dim, shards_of in pieces:
        heights = jax.random.uniform(jax.random.fold_in(jax.random.fold_in(own_key, 6), dim), (shards_of,), jnp.float32, low / len(pieces), largest / len(pieces))
        level = level * jnp.repeat(jnp.exp(heights), extent[dim] // shards_of).reshape((-1,) + (1,) * (len(extent) - 1 - dim))
    return level


def bell_draw(key, dims, width, limit, cuts=(), kind=jnp.bfloat16):
    loudness = shard_levels(key, dims, cuts, -0.22, 0.18) if cuts else 1.0
    drawn = jax.random.normal(key, dims, jnp.float32) * width * loudness
    return jnp.minimum(jnp.maximum(drawn, -limit), limit).astype(kind)


def bell_draw_with(stream_key, extent, spread, bound, pieces, heavy, kind=jnp.bfloat16):
    values = spread * jax.random.normal(stream_key, extent, jnp.float32)
    if pieces:
        values = values * shard_levels(stream_key, extent, pieces, -0.22, 0.18)
    return jnp.clip(spiked(values, jax.random.fold_in(stream_key, 3), *heavy), -bound, bound).astype(kind)


def setup_inputs(seed: int = 0) -> dict:
    streams_of = jax.random.split(jax.random.key(seed), 6)
    return {
        "queries": draw_queries(jax.random.fold_in(streams_of[5], 71), 0),
        "keys": draw_keys(jax.random.fold_in(streams_of[5], 71), 0),
        "values": bell_draw(streams_of[2], (SEQUENCE_LENGTH, KEY_VALUE_HEADS * HEAD_SIZE), 1.0, 6.0, ((0, 256), (1, 2))),
        "residual": bell_draw(streams_of[3], (SEQUENCE_LENGTH, D), 1.0, 6.0, ((0, 256), (1, 2))),
        "out_weight": bell_draw_with(streams_of[4], (QUERY_HEADS * HEAD_SIZE, D), (QUERY_HEADS * HEAD_SIZE) ** -0.5, 0.125, ((0, 2),), (0, 1, 2, 2.0)),
    }


def block_mask(local_rows, position):
    row_ids = lax.broadcasted_iota(jnp.int32, (local_rows, 5 * local_rows), 0)
    col_ids = lax.broadcasted_iota(jnp.int32, (local_rows, 5 * local_rows), 1)
    block_ids = col_ids // local_rows
    offset = col_ids - block_ids * local_rows
    distance = jnp.where(block_ids == 0, 0, jnp.left_shift(jnp.int32(1), jnp.maximum(block_ids - 1, 0)))
    return jnp.where(block_ids == 0, offset <= row_ids, position >= distance)

def attend(query_matrix, gathered_rows, position):
    local_rows = query_matrix.shape[0]
    queries_per_group = QUERY_HEADS // KEY_VALUE_HEADS
    reshaped_output = query_matrix.astype(jnp.float32).reshape(local_rows, KEY_VALUE_HEADS, queries_per_group, HEAD_SIZE)
    key_matrix = gathered_rows[0].astype(jnp.float32).reshape(-1, KEY_VALUE_HEADS, HEAD_SIZE)
    value_matrix = gathered_rows[1].astype(jnp.float32).reshape(-1, KEY_VALUE_HEADS, HEAD_SIZE)
    scores = jnp.einsum('qkgd,skd->kgqs', reshaped_output, key_matrix) / math.sqrt(HEAD_SIZE)
    scores = jnp.where(block_mask(local_rows, position), scores, -1e+30)
    row_peak = lax.optimization_barrier(jnp.max(scores, axis=-1, keepdims=True))
    raised = jnp.exp(scores - row_peak)
    weights = (raised / lax.optimization_barrier(jnp.sum(raised, axis=-1, keepdims=True))).astype(jnp.bfloat16)
    mixed = jnp.einsum('kgqs,skd->qkgd', weights.astype(jnp.float32), value_matrix)
    return mixed.reshape(local_rows, QUERY_HEADS * HEAD_SIZE).astype(jnp.bfloat16)

def reference(queries, keys, values, residual, out_weight):
    stacked = jnp.stack([keys, values])
    weight_wide = out_weight.astype(jnp.float32)

    def one_block(position):
        parts = []
        for distance in (0, 1, 2, 4, 8):
            source_block = (jnp.maximum(position - distance, 0) * TOK_DEV).astype(jnp.int32)
            parts.append(lax.dynamic_slice_in_dim(stacked, source_block, TOK_DEV, 1))
        gathered_rows = jnp.concatenate(parts, axis=1)
        first_row = (position * TOK_DEV).astype(jnp.int32)
        query_matrix = lax.dynamic_slice_in_dim(queries, first_row, TOK_DEV, 0)
        attended = attend(query_matrix, gathered_rows, position)
        projected = jnp.dot(attended.astype(jnp.float32), weight_wide)
        stream = lax.dynamic_slice_in_dim(residual, first_row, TOK_DEV, 0).astype(jnp.float32)
        return (stream + projected).astype(jnp.bfloat16)
    blocks_out = lax.map(one_block, jnp.arange(N_CTX, dtype=jnp.int32))
    return blocks_out.reshape(N_CTX * TOK_DEV, D)
```

```python
import functools
import math

import jax
import jax.numpy as jnp
from jax import lax
from jax.experimental import pallas as pl
from jax.experimental.pallas import tpu as pltpu
from jax.sharding import PartitionSpec as P


HEAD = 128
SCALE = math.log2(math.e) / math.sqrt(HEAD)
MIB = 1 << 20
F32, BF16 = jnp.float32, jnp.bfloat16


def route(axis, target):
    n = lax.axis_size(axis)
    return [(i, target(i)) for i in range(n) if target(i) is not None and 0 <= target(i) < n]


def head_step(q, blocks, prev, group, rows):
    tile = 128
    ones = jnp.ones((rows, HEAD), BF16)
    wide = [jnp.concatenate([v, ones], axis=1) for _, v, _, _ in blocks]
    units = [(j, r) for j in range(group) for r in range(0, rows, tile)]

    def seen(kind, r):
        return r + tile if kind == "own" else rows

    def scores_of(unit):
        j, r = unit
        qj = q[r : r + tile, j * HEAD : (j + 1) * HEAD]
        out = []
        for k, _, kind, _ in blocks:
            n = seen(kind, r)
            s = lax.dot_general(qj, k[:n], (((1,), (1,)), ((), ())), preferred_element_type=F32)
            if kind == "own":
                row = lax.broadcasted_iota(jnp.int32, (tile, n), 0) + r
                s = jnp.where(lax.broadcasted_iota(jnp.int32, (tile, n), 1) <= row, s, -1e30)
            out.append(s)
        return out

    ahead = scores_of(units[0])
    for i, (j, r) in enumerate(units):
        scores = ahead
        if True and i + 1 < len(units):
            ahead = scores_of(units[i + 1])
        tops = []
        for s, (_, _, kind, valid) in zip(scores, blocks):
            top = s[:, :HEAD]
            for t in range(HEAD, s.shape[1], HEAD):
                top = jnp.maximum(top, s[:, t : t + HEAD])
            tops.append(top if kind == "own" else jnp.where(valid, top, -1e30))
        top = functools.reduce(jnp.maximum, tops)
        m = jnp.broadcast_to(jnp.max(top, axis=1, keepdims=True), top.shape)
        if prev is not None:
            acc0, m0, l0 = prev(j, pl.ds(r, tile))
            m = jnp.maximum(m, m0)
        mc = m * SCALE
        total = None
        for s, w, (_, _, kind, valid) in zip(scores, wide, blocks):
            shift = mc if kind == "own" else jnp.where(valid, mc, 1e30)
            n = s.shape[1]
            p = jnp.exp2(s * SCALE - jnp.concatenate([shift] * (n // HEAD), axis=1)).astype(BF16)
            part = jnp.dot(p, w[:n], preferred_element_type=F32)
            total = part if total is None else total + part
        acc, l = total[:, :HEAD], total[:, HEAD:]
        if prev is not None:
            alpha = jnp.exp2(m0 * SCALE - mc)
            acc = acc + alpha * acc0
            l = l + alpha * l0
        yield j, pl.ds(r, tile), (acc, m, l)
        if not True and i + 1 < len(units):
            ahead = scores_of(units[i + 1])


def columns(start, size):
    return pl.ds(pl.multiple_of(start, HEAD), size)


def reader(state):
    return lambda j, r: tuple(ref[r, j * HEAD : (j + 1) * HEAD] for ref in state)


def part_kernel(distances, has_prev, fetch, *refs):
    refs = list(refs)
    q_ref = refs.pop(0)
    pairs = [(refs.pop(0), refs.pop(0)) for _ in distances]
    prev_refs = [refs.pop(0) for _ in range(3)] if has_prev else None
    w_hbm = refs.pop(0) if fetch else None
    state = [refs.pop(0) for _ in range(3)]
    w_vmem = refs.pop(0) if fetch else None
    g = pl.program_id(0)
    rows = q_ref.shape[0]
    group = q_ref.shape[1] // HEAD
    if fetch:
        copy = pltpu.make_async_copy(w_hbm, w_vmem, refs.pop(0))
        pl.when(g == 0)(copy.start)
    position = lax.axis_index("ctx")
    blocks = [
        (k[...], v[...], "own" if d == 0 else "far", position >= d)
        for (k, v), d in zip(pairs, distances)
    ]
    prev = reader(prev_refs) if has_prev else None
    for j, r, new in head_step(q_ref[...], blocks, prev, group, rows):
        for ref, value in zip(state, new):
            ref[r, j * HEAD : (j + 1) * HEAD] = value
    if fetch:
        pl.when(g == pl.num_programs(0) - 1)(copy.wait)


def last_kernel(distances, q_ref, *refs):
    refs = list(refs)
    pairs = [(refs.pop(0), refs.pop(0)) for _ in distances]
    *state, att_ref = refs
    rows = q_ref.shape[0]
    group = q_ref.shape[1] // HEAD
    position = lax.axis_index("ctx")
    blocks = [(k[...], v[...], "far", position >= d) for (k, v), d in zip(pairs, distances)]
    for j, r, (acc, _, l) in head_step(q_ref[...], blocks, reader(state), group, rows):
        att_ref[r, j * HEAD : (j + 1) * HEAD] = (acc / l).astype(BF16)


def partner_kernel(att_ref, w_ref, send_ref):
    width = send_ref.shape[1]
    base = (1 - lax.axis_index("hid")) * width
    tile = 512

    @pl.loop(0, width // tile)
    def _(t):
        send_ref[:, columns(t * tile, tile)] = jnp.dot(
            att_ref[...], w_ref[:, columns(base + t * tile, tile)], preferred_element_type=F32
        ).astype(BF16)


def own_kernel(att_ref, w_ref, res_ref, out_ref):
    width = out_ref.shape[1]
    base = lax.axis_index("hid") * width
    tile = 512

    @pl.loop(0, width // tile)
    def _(t):
        here = columns(t * tile, tile)
        out_ref[:, here] = res_ref[:, here].astype(F32) + jnp.dot(
            att_ref[...], w_ref[:, columns(base + t * tile, tile)], preferred_element_type=F32
        )


def pack_kernel(a_ref, b_ref, out_ref, sems):
    rows = a_ref.shape[0]
    copies = [
        pltpu.make_async_copy(ref, out_ref.at[pl.ds(i * rows, rows)], sems.at[i])
        for i, ref in enumerate((a_ref, b_ref))
    ]
    for c in copies:
        c.start()
    for c in copies:
        c.wait()


def choose_kernel(both_ref, back_ref, two_ref, one_ref):
    rows = one_ref.shape[0]
    column = lax.rem(lax.axis_index("ctx"), 4)

    @pl.when(column < 2)
    def _():
        two_ref[...] = both_ref[...]

    @pl.when(column >= 2)
    def _():
        two_ref[...] = back_ref[...]

    @pl.when(column < 3)
    def _():
        one_ref[...] = both_ref[rows:]

    @pl.when(column == 3)
    def _():
        one_ref[...] = back_ref[rows:]


WHOLE = pl.BlockSpec(memory_space=pltpu.VMEM)
ANY = pl.BlockSpec(memory_space=pltpu.HBM)


def kv_specs(source, rows):
    if isinstance(source, tuple):
        return list(source), [pl.BlockSpec((rows, HEAD), lambda g: (0, g))] * 2
    return [source, source], [
        pl.BlockSpec((rows, HEAD), lambda g: (0, g)),
        pl.BlockSpec((rows, HEAD), lambda g: (1, g)),
    ]


def packed(keys, values):
    rows, width = keys.shape
    return pl.pallas_call(
        pack_kernel,
        out_shape=pltpu.VMEM((2 * rows, width), keys.dtype),
        in_specs=[ANY, ANY],
        out_specs=WHOLE,
        scratch_shapes=[pltpu.SemaphoreType.DMA((2,))],
        compiler_params=pltpu.CompilerParams(vmem_limit_bytes=4 * MIB),
    )(*(pltpu.with_memory_space_constraint(a, pltpu.HBM) for a in (keys, values)))


def chosen(both, back):
    rows, width = both.shape
    return pl.pallas_call(
        choose_kernel,
        out_shape=(pltpu.VMEM(both.shape, both.dtype), pltpu.VMEM((rows // 2, width), both.dtype)),
        in_specs=[WHOLE, WHOLE],
        out_specs=(WHOLE, WHOLE),
        compiler_params=pltpu.CompilerParams(vmem_limit_bytes=4 * MIB),
    )(both, back)


def cost(rows, width, blocks, extra=0):
    return pl.CostEstimate(
        flops=4 * rows * width * rows * blocks + extra,
        bytes_accessed=2 * MIB,
        transcendentals=rows * (width // HEAD) * rows * blocks,
    )


def attend(q, sources, distances, prev=None, weight=None, last=False, limit=8):
    rows, width = q.shape
    heads = width // (4 * HEAD)
    wide = pl.BlockSpec((rows, 4 * HEAD), lambda g: (0, g))
    args, specs = [q], [wide]
    for s in sources:
        a, sp = kv_specs(s, rows)
        args += a
        specs += sp
    if prev is not None:
        args += list(prev)
        specs += [wide] * 3
    if last:
        outs, out_specs = [pltpu.VMEM((rows, width), BF16)], [wide]
        body = functools.partial(last_kernel, distances)
    else:
        outs, out_specs = [pltpu.VMEM((rows, width), F32)] * 3, [wide] * 3
        body = functools.partial(part_kernel, distances, prev is not None, weight is not None)
    scratch = []
    if weight is not None:
        args.append(pltpu.with_memory_space_constraint(weight, pltpu.HBM))
        specs.append(ANY)
        outs.append(pltpu.VMEM(weight.shape, weight.dtype))
        out_specs.append(WHOLE)
        scratch.append(pltpu.SemaphoreType.DMA(()))
    return pl.pallas_call(
        body,
        grid=(heads,),
        out_shape=tuple(outs),
        in_specs=specs,
        out_specs=tuple(out_specs),
        scratch_shapes=scratch,
        cost_estimate=cost(rows, width, len(sources)),
        compiler_params=pltpu.CompilerParams(vmem_limit_bytes=limit * MIB),
    )(*args)


def project_partner(att, weight, limit=8):
    rows, half = att.shape[0], weight.shape[1] // 2
    return pl.pallas_call(
        partner_kernel,
        out_shape=pltpu.VMEM((rows, half), BF16),
        in_specs=[WHOLE] * 2,
        out_specs=WHOLE,
        cost_estimate=pl.CostEstimate(
            flops=2 * rows * weight.shape[0] * half, bytes_accessed=2 * MIB, transcendentals=0
        ),
        compiler_params=pltpu.CompilerParams(vmem_limit_bytes=limit * MIB),
    )(att, weight)


def project_own(att, weight, residual, limit=8):
    rows, half = residual.shape
    return pl.pallas_call(
        own_kernel,
        out_shape=pltpu.VMEM((rows, half), F32),
        in_specs=[WHOLE] * 3,
        out_specs=WHOLE,
        cost_estimate=pl.CostEstimate(
            flops=2 * rows * weight.shape[0] * half, bytes_accessed=2 * MIB, transcendentals=0
        ),
        compiler_params=pltpu.CompilerParams(vmem_limit_bytes=limit * MIB),
    )(att, weight, residual)


def on_device(queries, keys, values, residual, out_weight):
  up = route("ctx", lambda i: i + 4)
  ring1 = route("ctx", lambda i: i // 4 * 4 + (i + 1) % 4)
  ring2 = route("ctx", lambda i: i // 4 * 4 + (i + 2) % 4)
  both = packed(keys, values)
  back4 = lax.ppermute(both, "ctx", up)
  key1 = lax.ppermute(keys, "ctx", route("ctx", lambda i: i + 1))
  *state, weight = attend(queries, [(keys, values)], (0,), weight=out_weight)
  back8 = lax.ppermute(back4, "ctx", up)
  two, one = chosen(both, back4)
  back2 = lax.ppermute(two, "ctx", ring2)
  value1 = lax.ppermute(one, "ctx", ring1)
  state = attend(queries, [back4], (4,), state)
  (attended,) = attend(queries, [(key1, value1), back2, back8], (1, 2, 8), state, last=True)
  sent = project_partner(attended, weight)
  received = lax.ppermute(sent, "hid", [(0, 1), (1, 0)])
  kept = project_own(attended, weight, residual)
  return (kept + received.astype(F32)).astype(BF16)


def solution(mesh):
    return jax.shard_map(
        on_device,
        mesh=mesh,
        in_specs=(P("ctx", "hid"), P("ctx", "hid"), P("ctx", "hid"), P("ctx", "hid"), P("hid", None)),
        out_specs=P("ctx", "hid"),
        check_vma=False,
    )
```

```python
import functools
import math

import jax
import jax.numpy as jnp
from jax import lax
from jax.experimental import pallas as pl
from jax.experimental.pallas import tpu as pltpu
from jax.sharding import PartitionSpec as P


HEAD = 128
GROUP = 4
SCALE = math.log2(math.e) / math.sqrt(HEAD)
MIB = 1 << 20
F32, BF16 = jnp.float32, jnp.bfloat16
WHOLE = pl.BlockSpec(memory_space=pltpu.VMEM)
IN_HBM = pl.BlockSpec(memory_space=pltpu.HBM)


def params(limit):
    return pltpu.CompilerParams(vmem_limit_bytes=limit * MIB)


def hbm(x):
    return pltpu.with_memory_space_constraint(x, pltpu.HBM)


def route(axis, target):
    n = lax.axis_size(axis)
    return [(i, target(i)) for i in range(n) if 0 <= target(i) < n]


def columns(start, size):
    return pl.ds(pl.multiple_of(start, HEAD), size)


def softmax_units(q_ref, g, blocks, prev):
    rows, tile = q_ref.shape[0], 128
    units = [(j, r) for j in range(GROUP) for r in range(0, rows, tile)]

    def scores_of(unit):
        j, r = unit
        at = (g * GROUP + j) * HEAD
        q = q_ref[r : r + tile, at : at + HEAD]
        out = []
        for key, _, own in blocks:
            n = r + tile if own else rows
            s = lax.dot_general(q, key[:n], (((1,), (1,)), ((), ())), preferred_element_type=F32)
            if own:
                row = lax.broadcasted_iota(jnp.int32, (tile, n), 0) + r
                s = jnp.where(lax.broadcasted_iota(jnp.int32, (tile, n), 1) <= row, s, -1e30)
            out.append(s)
        return jnp.concatenate(out, axis=1)

    ahead = scores_of(units[0])
    for i, (j, r) in enumerate(units):
        s = ahead
        where = (pl.ds(r, tile), pl.ds((g * GROUP + j) * HEAD, HEAD))
        top = functools.reduce(
            jnp.maximum, [s[:, t : t + HEAD] for t in range(0, s.shape[1], HEAD)]
        )
        m = jnp.broadcast_to(jnp.max(top, axis=1, keepdims=True), top.shape)
        if prev is not None:
            acc0, m0, l0 = (ref[where] for ref in prev)
            m = jnp.maximum(m, m0)
        mc = m * SCALE
        p = jnp.exp2(s * SCALE - jnp.concatenate([mc] * (s.shape[1] // HEAD), axis=1)).astype(BF16)
        values = jnp.concatenate([w[: r + tile if own else rows] for _, w, own in blocks], axis=0)
        total = jnp.dot(p, values, preferred_element_type=F32)
        acc, l = total[:, :HEAD], total[:, HEAD:]
        if prev is not None:
            alpha = jnp.exp2(m0 * SCALE - mc)
            acc = acc + alpha * acc0
            l = l + alpha * l0
        yield where, (acc, m, l)
        if i + 1 < len(units):
            ahead = scores_of(units[i + 1])


def head_blocks(g, pairs, distances, first_ref):
    at = pl.ds(g * HEAD, HEAD)
    rows = first_ref.shape[0]
    position = lax.axis_index("ctx")
    out = []
    for (k_ref, v_ref), d in zip(pairs, distances):
        k, v, ones = k_ref[:, at], v_ref[:, at], jnp.ones((rows, HEAD), BF16)
        if d:
            there = position >= d
            first = jnp.broadcast_to(first_ref[0:1, at], k.shape)
            k = jnp.where(there, k, first)
            v = jnp.where(there, v, jnp.zeros_like(v))
            ones = jnp.where(there, ones, jnp.zeros_like(ones))
        out.append((k, jnp.concatenate([v, ones], axis=1), d == 0))
    return out


def split_pairs(refs, stacked):
    pairs = []
    for both in stacked:
        if both:
            ref = refs.pop(0)
            rows = ref.shape[0] // 2
            pairs.append((ref.at[pl.ds(0, rows)], ref.at[pl.ds(rows, rows)]))
        else:
            pairs.append((refs.pop(0), refs.pop(0)))
    return pairs


def own_kernel(q_ref, k_ref, v_ref, w_hbm, acc_ref, m_ref, l_ref, w_ref, sem):
    copy = pltpu.make_async_copy(w_hbm, w_ref, sem)
    copy.start()
    for g in range(k_ref.shape[1] // HEAD):
        blocks = head_blocks(g, [(k_ref, v_ref)], (0,), k_ref)
        for where, new in softmax_units(q_ref, g, blocks, None):
            for ref, value in zip((acc_ref, m_ref, l_ref), new):
                ref[where] = value
    copy.wait()


def middle_kernel(distances, stacked, q_ref, first_ref, *refs):
    refs = list(refs)
    pairs = split_pairs(refs, stacked)
    prev, state = refs[:3], refs[3:]
    for g in range(first_ref.shape[1] // HEAD):
        blocks = head_blocks(g, pairs, distances, first_ref)
        for where, new in softmax_units(q_ref, g, blocks, prev):
            for ref, value in zip(state, new):
                ref[where] = value


def last_kernel(distances, stacked, q_ref, first_ref, *refs):
    refs = list(refs)
    pairs = split_pairs(refs, stacked)
    prev, (w_ref, att_ref, send_ref) = refs[:3], refs[3:]
    for g in range(first_ref.shape[1] // HEAD):
        blocks = head_blocks(g, pairs, distances, first_ref)
        for where, (acc, _, l) in softmax_units(q_ref, g, blocks, prev):
            att_ref[where] = (acc / l).astype(BF16)
    width = send_ref.shape[1]
    base = (1 - lax.axis_index("hid")) * width
    tile = 512

    @pl.loop(0, width // tile)
    def _(t):
        send_ref[:, columns(t * tile, tile)] = jnp.dot(
            att_ref[...], w_ref[:, columns(base + t * tile, tile)], preferred_element_type=F32
        ).astype(BF16)


def kept_kernel(att_ref, w_ref, res_ref, out_ref):
    width = out_ref.shape[1]
    base = lax.axis_index("hid") * width
    tile = 512

    @pl.loop(0, width // tile)
    def _(t):
        here = columns(t * tile, tile)
        out_ref[:, here] = res_ref[:, here].astype(F32) + jnp.dot(
            att_ref[...], w_ref[:, columns(base + t * tile, tile)], preferred_element_type=F32
        )


def stage_kernel(*refs):
    n = len(refs) // 2
    *refs, sems = refs
    copies = [pltpu.make_async_copy(refs[i], refs[n + i], sems.at[i]) for i in range(n)]
    for c in copies:
        c.start()
    for c in copies:
        c.wait()


def choose(limit, mine_ref, back_ref, out_ref):
    column = lax.rem(lax.axis_index("ctx"), 4)

    @pl.when(column < limit)
    def _():
        out_ref[...] = mine_ref[...]

    @pl.when(column >= limit)
    def _():
        out_ref[...] = back_ref[...]


def staged(*arrays):
    return pl.pallas_call(
        stage_kernel,
        out_shape=tuple(pltpu.VMEM(a.shape, a.dtype) for a in arrays),
        in_specs=[IN_HBM] * len(arrays),
        out_specs=(WHOLE,) * len(arrays),
        scratch_shapes=[pltpu.SemaphoreType.DMA((len(arrays),))],
        compiler_params=params(2),
    )(*map(hbm, arrays))


def chosen_keys(mine, back):
    def kernel(mine_ref, back_ref, out_ref):
        choose(2, mine_ref, back_ref, out_ref)

    return pl.pallas_call(
        kernel,
        out_shape=pltpu.VMEM(mine.shape, mine.dtype),
        in_specs=[WHOLE] * 2,
        out_specs=WHOLE,
        compiler_params=params(2),
    )(mine, back)


def chosen_values(mine, back_keys, back):
    rows, width = mine.shape

    def kernel(mine_ref, back_keys_ref, back_ref, two_ref, one_ref, both_ref):
        choose(2, mine_ref, back_ref, two_ref)
        choose(3, mine_ref, back_ref, one_ref)
        both_ref[0:rows] = back_keys_ref[...]
        both_ref[rows:] = back_ref[...]

    one = pltpu.VMEM(mine.shape, mine.dtype)
    return pl.pallas_call(
        kernel,
        out_shape=(one, one, pltpu.VMEM((2 * rows, width), mine.dtype)),
        in_specs=[WHOLE] * 3,
        out_specs=(WHOLE,) * 3,
        compiler_params=params(2),
    )(mine, back_keys, back)


def estimate(rows, width, blocks, more=0):
    return pl.CostEstimate(
        flops=4 * rows * width * rows * blocks + more,
        bytes_accessed=2 * MIB,
        transcendentals=rows * (width // HEAD) * rows * blocks,
    )


def state_of(q):
    return [pltpu.VMEM(q.shape, F32)] * 3


def attend_own(q, keys, values, weight):
    return pl.pallas_call(
        own_kernel,
        out_shape=(*state_of(q), pltpu.VMEM(weight.shape, weight.dtype)),
        in_specs=[WHOLE] * 3 + [IN_HBM],
        out_specs=(WHOLE,) * 4,
        scratch_shapes=[pltpu.SemaphoreType.DMA(())],
        cost_estimate=estimate(*q.shape, 1),
        compiler_params=params(8),
    )(q, keys, values, hbm(weight))


def flat(sources):
    stacked = tuple(not isinstance(s, tuple) for s in sources)
    return stacked, [a for s in sources for a in (s if isinstance(s, tuple) else (s,))]


def attend_middle(q, first, sources, distances, state):
    stacked, arrays = flat(sources)
    return pl.pallas_call(
        functools.partial(middle_kernel, distances, stacked),
        out_shape=tuple(state_of(q)),
        in_specs=[WHOLE] * (5 + len(arrays)),
        out_specs=(WHOLE,) * 3,
        cost_estimate=estimate(*q.shape, len(sources)),
        compiler_params=params(8),
    )(q, first, *arrays, *state)


def attend_last(q, first, sources, distances, state, weight):
    stacked, arrays = flat(sources)
    rows, width = q.shape
    half = weight.shape[1] // 2
    return pl.pallas_call(
        functools.partial(last_kernel, distances, stacked),
        out_shape=(pltpu.VMEM(q.shape, BF16), pltpu.VMEM((rows, half), BF16)),
        in_specs=[WHOLE] * (6 + len(arrays)),
        out_specs=(WHOLE,) * 2,
        cost_estimate=estimate(rows, width, len(sources), 2 * rows * width * half),
        compiler_params=params(8),
    )(q, first, *arrays, *state, weight)


def project_kept(att, weight, residual):
    rows, half = residual.shape
    return pl.pallas_call(
        kept_kernel,
        out_shape=pltpu.VMEM((rows, half), F32),
        in_specs=[WHOLE] * 3,
        out_specs=WHOLE,
        cost_estimate=pl.CostEstimate(
            flops=2 * rows * weight.shape[0] * half, bytes_accessed=2 * MIB, transcendentals=0
        ),
        compiler_params=params(4),
    )(att, weight, residual)


def on_device(queries, keys, values, residual, out_weight):
    up = route("ctx", lambda i: i + 4)
    ring1 = route("ctx", lambda i: i // 4 * 4 + (i + 1) % 4)
    ring2 = route("ctx", lambda i: i // 4 * 4 + (i + 2) % 4)
    keys4 = lax.ppermute(keys, "ctx", up)
    values4 = lax.ppermute(values, "ctx", up)
    keys1 = lax.ppermute(keys, "ctx", route("ctx", lambda i: i + 1))
    q, k, v = staged(queries, keys, values)
    two = chosen_keys(k, keys4)
    keys2 = lax.ppermute(two, "ctx", ring2)
    two, one, both = chosen_values(v, keys4, values4)
    values2 = lax.ppermute(two, "ctx", ring2)
    back8 = lax.ppermute(both, "ctx", up)
    values1 = lax.ppermute(one, "ctx", ring1)
    *state, weight = attend_own(q, k, v, out_weight)
    state = attend_middle(q, k, [(keys4, values4)], (4,), state)
    attended, sent = attend_last(
        q, k, [(keys1, values1), (keys2, values2), back8], (1, 2, 8), state, weight
    )
    received = lax.ppermute(sent, "hid", [(0, 1), (1, 0)])
    kept = project_kept(attended, weight, residual)
    return (kept + received.astype(F32)).astype(BF16)


def solution(mesh):
    return jax.shard_map(
        on_device,
        mesh=mesh,
        in_specs=(P("ctx", "hid"), P("ctx", "hid"), P("ctx", "hid"), P("ctx", "hid"), P("hid", None)),
        out_specs=P("ctx", "hid"),
        check_vma=False,
    )
```

```python
import functools
import math

import jax
import jax.numpy as jnp
from jax import lax
from jax.experimental import pallas as pl
from jax.experimental.pallas import tpu as pltpu
from jax.sharding import PartitionSpec as P


HEAD = 128
GROUP = 4
SCALE = math.log2(math.e) / math.sqrt(HEAD)
MIB = 1 << 20
F32, BF16 = jnp.float32, jnp.bfloat16
WHOLE = pl.BlockSpec(memory_space=pltpu.VMEM)
IN_HBM = pl.BlockSpec(memory_space=pltpu.HBM)


def params(limit):
    return pltpu.CompilerParams(vmem_limit_bytes=limit * MIB)


def hbm(x):
    return pltpu.with_memory_space_constraint(x, pltpu.HBM)


def route(axis, target):
    n = lax.axis_size(axis)
    return [(i, target(i)) for i in range(n) if 0 <= target(i) < n]


def columns(start, size):
    return pl.ds(pl.multiple_of(start, HEAD), size)


def softmax_units(q_ref, g, blocks, prev):
    rows, tile = q_ref.shape[0], 128
    units = [(j, r) for j in range(GROUP) for r in range(0, rows, tile)]

    def scores_of(unit):
        j, r = unit
        at = (g * GROUP + j) * HEAD
        q = q_ref[r : r + tile, at : at + HEAD]
        out = []
        for key, _, own in blocks:
            n = r + tile if own else rows
            s = lax.dot_general(q, key[:n], (((1,), (1,)), ((), ())), preferred_element_type=F32)
            if own:
                row = lax.broadcasted_iota(jnp.int32, (tile, n), 0) + r
                s = jnp.where(lax.broadcasted_iota(jnp.int32, (tile, n), 1) <= row, s, -1e30)
            out.append(s)
        return jnp.concatenate(out, axis=1)

    ahead = scores_of(units[0])
    for i, (j, r) in enumerate(units):
        s = ahead
        where = (pl.ds(r, tile), pl.ds((g * GROUP + j) * HEAD, HEAD))
        top = functools.reduce(
            jnp.maximum, [s[:, t : t + HEAD] for t in range(0, s.shape[1], HEAD)]
        )
        m = jnp.broadcast_to(jnp.max(top, axis=1, keepdims=True), top.shape)
        if prev is not None:
            acc0, m0, l0 = (ref[where] for ref in prev)
            m = jnp.maximum(m, m0)
        mc = m * SCALE
        p = jnp.exp2(s * SCALE - jnp.concatenate([mc] * (s.shape[1] // HEAD), axis=1)).astype(BF16)
        values = jnp.concatenate([w[: r + tile if own else rows] for _, w, own in blocks], axis=0)
        total = jnp.dot(p, values, preferred_element_type=F32)
        acc, l = total[:, :HEAD], total[:, HEAD:]
        if prev is not None:
            alpha = jnp.exp2(m0 * SCALE - mc)
            acc = acc + alpha * acc0
            l = l + alpha * l0
        yield where, (acc, m, l)
        if i + 1 < len(units):
            ahead = scores_of(units[i + 1])


def head_blocks(g, pairs, distances, first_ref):
    at = pl.ds(g * HEAD, HEAD)
    rows = first_ref.shape[0]
    position = lax.axis_index("ctx")
    out = []
    for (k_ref, v_ref), d in zip(pairs, distances):
        k, v, ones = k_ref[:, at], v_ref[:, at], jnp.ones((rows, HEAD), BF16)
        if d:
            there = position >= d
            first = jnp.broadcast_to(first_ref[0:1, at], k.shape)
            k = jnp.where(there, k, first)
            v = jnp.where(there, v, jnp.zeros_like(v))
            ones = jnp.where(there, ones, jnp.zeros_like(ones))
        out.append((k, jnp.concatenate([v, ones], axis=1), d == 0))
    return out


def split_pairs(refs, stacked):
    pairs = []
    for both in stacked:
        if both:
            ref = refs.pop(0)
            rows = ref.shape[0] // 2
            pairs.append((ref.at[pl.ds(0, rows)], ref.at[pl.ds(rows, rows)]))
        else:
            pairs.append((refs.pop(0), refs.pop(0)))
    return pairs


def part_kernel(distances, has_prev, half, q_ref, first_ref, *refs):
    refs = list(refs)
    pairs = [(refs.pop(0), refs.pop(0)) for _ in distances]
    prev = [refs.pop(0) for _ in range(3)] if has_prev else None
    w_hbm, *state, w_ref, sems = refs
    size = w_ref.shape[0] // sems.shape[0]
    copies = []
    for i in range(sems.shape[0]):
        source = w_hbm.at[pl.ds(half * w_ref.shape[0] + i * size, size)]
        copies.append(pltpu.make_async_copy(source, w_ref.at[pl.ds(i * size, size)], sems.at[i]))
        copies[-1].start()
    for g in range(first_ref.shape[1] // HEAD):
        blocks = head_blocks(g, pairs, distances, first_ref)
        for where, new in softmax_units(q_ref, g, blocks, prev):
            for ref, value in zip(state, new):
                ref[where] = value
    for c in copies:
        c.wait()


def product(att_ref, weights, at):
    depth = weights[0].shape[0]
    return sum(
        jnp.dot(att_ref[:, i * depth : (i + 1) * depth], w[:, at], preferred_element_type=F32)
        for i, w in enumerate(weights)
    )


def last_kernel(distances, stacked, q_ref, first_ref, *refs):
    refs = list(refs)
    pairs = split_pairs(refs, stacked)
    prev, (*weights, att_ref, send_ref) = refs[:3], refs[3:]
    for g in range(first_ref.shape[1] // HEAD):
        blocks = head_blocks(g, pairs, distances, first_ref)
        for where, (acc, _, l) in softmax_units(q_ref, g, blocks, prev):
            att_ref[where] = (acc / l).astype(BF16)
    width, tile = send_ref.shape[1], 512
    base = (1 - lax.axis_index("hid")) * width

    @pl.loop(0, width // tile)
    def _(t):
        send_ref[:, columns(t * tile, tile)] = product(
            att_ref, weights, columns(base + t * tile, tile)
        ).astype(BF16)


def kept_kernel(att_ref, low_ref, high_ref, res_ref, out_ref):
    width, tile = out_ref.shape[1], 512
    base = lax.axis_index("hid") * width

    @pl.loop(0, width // tile)
    def _(t):
        here = columns(t * tile, tile)
        out_ref[:, here] = res_ref[:, here].astype(F32) + product(
            att_ref, (low_ref, high_ref), columns(base + t * tile, tile)
        )


def add_kernel(kept_ref, got_ref, out_hbm, buf_ref, sems):
    parts = sems.shape[0]
    size = buf_ref.shape[0] // parts
    copies = []
    for i in range(parts):
        at = pl.ds(i * size, size)
        buf_ref[at] = (kept_ref[at] + got_ref[at].astype(F32)).astype(BF16)
        copies.append(pltpu.make_async_copy(buf_ref.at[at], out_hbm.at[at], sems.at[i]))
        copies[-1].start()
    for c in copies:
        c.wait()


def stage_kernel(*refs):
    n = len(refs) // 2
    *refs, sems = refs
    copies = [pltpu.make_async_copy(refs[i], refs[n + i], sems.at[i]) for i in range(n)]
    for c in copies:
        c.start()
    for c in copies:
        c.wait()


def choose(limit, mine_ref, back_ref, out_ref):
    column = lax.rem(lax.axis_index("ctx"), 4)

    @pl.when(column < limit)
    def _():
        out_ref[...] = mine_ref[...]

    @pl.when(column >= limit)
    def _():
        out_ref[...] = back_ref[...]


def staged(*arrays):
    return pl.pallas_call(
        stage_kernel,
        out_shape=tuple(pltpu.VMEM(a.shape, a.dtype) for a in arrays),
        in_specs=[IN_HBM] * len(arrays),
        out_specs=(WHOLE,) * len(arrays),
        scratch_shapes=[pltpu.SemaphoreType.DMA((len(arrays),))],
        compiler_params=params(2),
    )(*map(hbm, arrays))


def chosen_keys(mine, back):
    def kernel(mine_ref, back_ref, out_ref):
        choose(2, mine_ref, back_ref, out_ref)

    return pl.pallas_call(
        kernel,
        out_shape=pltpu.VMEM(mine.shape, mine.dtype),
        in_specs=[WHOLE] * 2,
        out_specs=WHOLE,
        compiler_params=params(2),
    )(mine, back)


def chosen_values(mine, back_keys, back):
    rows, width = mine.shape

    def kernel(mine_ref, back_keys_ref, back_ref, two_ref, one_ref, both_ref):
        choose(2, mine_ref, back_ref, two_ref)
        choose(3, mine_ref, back_ref, one_ref)
        both_ref[0:rows] = back_keys_ref[...]
        both_ref[rows:] = back_ref[...]

    one = pltpu.VMEM(mine.shape, mine.dtype)
    return pl.pallas_call(
        kernel,
        out_shape=(one, one, pltpu.VMEM((2 * rows, width), mine.dtype)),
        in_specs=[WHOLE] * 3,
        out_specs=(WHOLE,) * 3,
        compiler_params=params(2),
    )(mine, back_keys, back)


def estimate(rows, width, blocks, more=0):
    return pl.CostEstimate(
        flops=4 * rows * width * rows * blocks + more,
        bytes_accessed=2 * MIB,
        transcendentals=rows * (width // HEAD) * rows * blocks,
    )


def state_of(q):
    return [pltpu.VMEM(q.shape, F32)] * 3


def attend_part(q, first, pairs, distances, state, weight, half):
    arrays = [a for pair in pairs for a in pair]
    rows = pltpu.VMEM((weight.shape[0] // 2, weight.shape[1]), weight.dtype)
    return pl.pallas_call(
        functools.partial(part_kernel, distances, bool(state), half),
        out_shape=(*state_of(q), rows),
        in_specs=[WHOLE] * (2 + len(arrays) + len(state)) + [IN_HBM],
        out_specs=(WHOLE,) * 4,
        scratch_shapes=[pltpu.SemaphoreType.DMA((1,))],
        cost_estimate=estimate(*q.shape, len(pairs)),
        compiler_params=params(8),
    )(q, first, *arrays, *state, hbm(weight))


def flat(sources):
    stacked = tuple(not isinstance(s, tuple) for s in sources)
    return stacked, [a for s in sources for a in (s if isinstance(s, tuple) else (s,))]


def attend_last(q, first, sources, distances, state, weights):
    stacked, arrays = flat(sources)
    rows, width = q.shape
    half = weights[0].shape[1] // 2
    return pl.pallas_call(
        functools.partial(last_kernel, distances, stacked),
        out_shape=(pltpu.VMEM(q.shape, BF16), pltpu.VMEM((rows, half), BF16)),
        in_specs=[WHOLE] * (7 + len(arrays)),
        out_specs=(WHOLE,) * 2,
        cost_estimate=estimate(rows, width, len(sources), 2 * rows * width * half),
        compiler_params=params(8),
    )(q, first, *arrays, *state, *weights)


def project_kept(att, weights, residual):
    rows, half = residual.shape
    return pl.pallas_call(
        kept_kernel,
        out_shape=pltpu.VMEM((rows, half), F32),
        in_specs=[WHOLE] * 4,
        out_specs=WHOLE,
        cost_estimate=pl.CostEstimate(
            flops=2 * rows * att.shape[1] * half, bytes_accessed=2 * MIB, transcendentals=0
        ),
        compiler_params=params(4),
    )(att, *weights, residual)


def added(kept, received):
    return pl.pallas_call(
        add_kernel,
        out_shape=jax.ShapeDtypeStruct(received.shape, received.dtype),
        in_specs=[WHOLE] * 2,
        out_specs=IN_HBM,
        scratch_shapes=[
            pltpu.VMEM(received.shape, received.dtype),
            pltpu.SemaphoreType.DMA((4,)),
        ],
        compiler_params=params(4),
    )(kept, received)


def on_device(queries, keys, values, residual, out_weight):
    up = route("ctx", lambda i: i + 4)
    ring1 = route("ctx", lambda i: i // 4 * 4 + (i + 1) % 4)
    ring2 = route("ctx", lambda i: i // 4 * 4 + (i + 2) % 4)
    keys4 = lax.ppermute(keys, "ctx", up)
    values4 = lax.ppermute(values, "ctx", up)
    keys1 = lax.ppermute(keys, "ctx", route("ctx", lambda i: i + 1))
    q, k, v = staged(queries, keys, values)
    two = chosen_keys(k, keys4)
    keys2 = lax.ppermute(two, "ctx", ring2)
    two, one, both = chosen_values(v, keys4, values4)
    values2 = lax.ppermute(two, "ctx", ring2)
    back8 = lax.ppermute(both, "ctx", up)
    values1 = lax.ppermute(one, "ctx", ring1)
    *state, low = attend_part(
        q, k, [(k, v), (keys4, values4)], (0, 4), (), out_weight, 0
    )
    *state, high = attend_part(q, k, [(keys2, values2)], (2,), state, out_weight, 1)
    attended, sent = attend_last(q, k, [(keys1, values1), back8], (1, 8), state, (low, high))
    received = lax.ppermute(sent, "hid", [(0, 1), (1, 0)])
    kept = project_kept(attended, (low, high), residual)
    return added(kept, received)


def solution(mesh):
    return jax.shard_map(
        on_device,
        mesh=mesh,
        in_specs=(P("ctx", "hid"), P("ctx", "hid"), P("ctx", "hid"), P("ctx", "hid"), P("hid", None)),
        out_specs=P("ctx", "hid"),
        check_vma=False,
    )
```

```python
import functools
import math

import jax
import jax.numpy as jnp
from jax import lax
from jax.experimental import pallas as pl
from jax.experimental.pallas import tpu as pltpu
from jax.sharding import PartitionSpec as P


HEAD = 128
GROUP = 4
SCALE = math.log2(math.e) / math.sqrt(HEAD)
MIB = 1 << 20
F32, BF16 = jnp.float32, jnp.bfloat16
WHOLE = pl.BlockSpec(memory_space=pltpu.VMEM)
IN_HBM = pl.BlockSpec(memory_space=pltpu.HBM)


def params(limit):
    return pltpu.CompilerParams(vmem_limit_bytes=limit * MIB)


def hbm(x):
    return pltpu.with_memory_space_constraint(x, pltpu.HBM)


def route(axis, target):
    n = lax.axis_size(axis)
    return [(i, target(i)) for i in range(n) if 0 <= target(i) < n]


def columns(start, size):
    return pl.ds(pl.multiple_of(start, HEAD), size)


def softmax_units(q_ref, g, blocks, prev):
    rows, tile = q_ref.shape[0], 128
    units = [(j, r) for j in range(GROUP) for r in range(0, rows, tile)]

    def scores_of(unit):
        j, r = unit
        at = (g * GROUP + j) * HEAD
        q = q_ref[r : r + tile, at : at + HEAD]
        out = []
        for key, _, own in blocks:
            n = r + tile if own else rows
            s = lax.dot_general(q, key[:n], (((1,), (1,)), ((), ())), preferred_element_type=F32)
            if own:
                row = lax.broadcasted_iota(jnp.int32, (tile, n), 0) + r
                s = jnp.where(lax.broadcasted_iota(jnp.int32, (tile, n), 1) <= row, s, -1e30)
            out.append(s)
        return jnp.concatenate(out, axis=1)

    ahead = scores_of(units[0])
    for i, (j, r) in enumerate(units):
        s = ahead
        where = (pl.ds(r, tile), pl.ds((g * GROUP + j) * HEAD, HEAD))
        top = functools.reduce(
            jnp.maximum, [s[:, t : t + HEAD] for t in range(0, s.shape[1], HEAD)]
        )
        m = jnp.broadcast_to(jnp.max(top, axis=1, keepdims=True), top.shape)
        if prev is not None:
            acc0, m0, l0 = (ref[where] for ref in prev)
            m = jnp.maximum(m, m0)
        mc = m * SCALE
        p = jnp.exp2(s * SCALE - jnp.concatenate([mc] * (s.shape[1] // HEAD), axis=1)).astype(BF16)
        values = jnp.concatenate([w[: r + tile if own else rows] for _, w, own in blocks], axis=0)
        total = jnp.dot(p, values, preferred_element_type=F32)
        acc, l = total[:, :HEAD], total[:, HEAD:]
        if prev is not None:
            alpha = jnp.exp2(m0 * SCALE - mc)
            acc = acc + alpha * acc0
            l = l + alpha * l0
        yield where, (acc, m, l)
        if i + 1 < len(units):
            ahead = scores_of(units[i + 1])


def head_blocks(g, pairs, distances, first_ref):
    at = pl.ds(g * HEAD, HEAD)
    rows = first_ref.shape[0]
    position = lax.axis_index("ctx")
    out = []
    for (k_ref, v_ref), d in zip(pairs, distances):
        k, v, ones = k_ref[:, at], v_ref[:, at], jnp.ones((rows, HEAD), BF16)
        if d:
            there = position >= d
            first = jnp.broadcast_to(first_ref[0:1, at], k.shape)
            k = jnp.where(there, k, first)
            v = jnp.where(there, v, jnp.zeros_like(v))
            ones = jnp.where(there, ones, jnp.zeros_like(ones))
        out.append((k, jnp.concatenate([v, ones], axis=1), d == 0))
    return out


def split_pairs(refs, stacked):
    pairs = []
    for both in stacked:
        if both:
            ref = refs.pop(0)
            rows = ref.shape[0] // 2
            pairs.append((ref.at[pl.ds(0, rows)], ref.at[pl.ds(rows, rows)]))
        else:
            pairs.append((refs.pop(0), refs.pop(0)))
    return pairs


def part_kernel(distances, has_prev, half, q_ref, first_ref, *refs):
    refs = list(refs)
    pairs = [(refs.pop(0), refs.pop(0)) for _ in distances]
    prev = [refs.pop(0) for _ in range(3)] if has_prev else None
    w_hbm, *state, w_ref, sems = refs
    size = w_ref.shape[0] // sems.shape[0]
    copies = []
    for i in range(sems.shape[0]):
        source = w_hbm.at[pl.ds(half * w_ref.shape[0] + i * size, size)]
        copies.append(pltpu.make_async_copy(source, w_ref.at[pl.ds(i * size, size)], sems.at[i]))
        copies[-1].start()
    for g in range(first_ref.shape[1] // HEAD):
        blocks = head_blocks(g, pairs, distances, first_ref)
        for where, new in softmax_units(q_ref, g, blocks, prev):
            for ref, value in zip(state, new):
                ref[where] = value
    for c in copies:
        c.wait()


def product(att_ref, weights, at):
    depth = weights[0].shape[0]
    return sum(
        jnp.dot(att_ref[:, i * depth : (i + 1) * depth], w[:, at], preferred_element_type=F32)
        for i, w in enumerate(weights)
    )


def last_kernel(distances, stacked, q_ref, first_ref, *refs):
    refs = list(refs)
    pairs = split_pairs(refs, stacked)
    prev, (att_ref,) = refs[:3], refs[3:]
    for g in range(first_ref.shape[1] // HEAD):
        blocks = head_blocks(g, pairs, distances, first_ref)
        for where, (acc, _, l) in softmax_units(q_ref, g, blocks, prev):
            att_ref[where] = (acc / l).astype(BF16)


def partner_kernel(att_ref, low_ref, high_ref, send_ref):
    width, tile = send_ref.shape[1], 512
    base = (1 - lax.axis_index("hid")) * width

    for t in range(width // tile):
        send_ref[:, columns(t * tile, tile)] = product(
            att_ref, (low_ref, high_ref), columns(base + t * tile, tile)
        ).astype(BF16)


def kept_kernel(att_ref, low_ref, high_ref, res_ref, out_ref):
    width, tile = out_ref.shape[1], 512
    base = lax.axis_index("hid") * width

    for t in range(width // tile):
        here = columns(t * tile, tile)
        out_ref[:, here] = res_ref[:, here].astype(F32) + product(
            att_ref, (low_ref, high_ref), columns(base + t * tile, tile)
        )


def add_kernel(kept_ref, got_ref, out_hbm, buf_ref, sems):
    parts = sems.shape[0]
    size = buf_ref.shape[0] // parts
    copies = []
    for i in range(parts):
        at = pl.ds(i * size, size)
        buf_ref[at] = (kept_ref[at] + got_ref[at].astype(F32)).astype(BF16)
        copies.append(pltpu.make_async_copy(buf_ref.at[at], out_hbm.at[at], sems.at[i]))
        copies[-1].start()
    for c in copies:
        c.wait()


def stage_kernel(*refs):
    n = len(refs) // 2
    *refs, sems = refs
    copies = [pltpu.make_async_copy(refs[i], refs[n + i], sems.at[i]) for i in range(n)]
    for c in copies:
        c.start()
    for c in copies:
        c.wait()


def choose(limit, mine_ref, back_ref, out_ref):
    column = lax.rem(lax.axis_index("ctx"), 4)

    @pl.when(column < limit)
    def _():
        out_ref[...] = mine_ref[...]

    @pl.when(column >= limit)
    def _():
        out_ref[...] = back_ref[...]


def staged(*arrays):
    return pl.pallas_call(
        stage_kernel,
        out_shape=tuple(pltpu.VMEM(a.shape, a.dtype) for a in arrays),
        in_specs=[IN_HBM] * len(arrays),
        out_specs=(WHOLE,) * len(arrays),
        scratch_shapes=[pltpu.SemaphoreType.DMA((len(arrays),))],
        compiler_params=params(2),
    )(*map(hbm, arrays))


def chosen_keys(mine, back):
    def kernel(mine_ref, back_ref, out_ref):
        choose(2, mine_ref, back_ref, out_ref)

    return pl.pallas_call(
        kernel,
        out_shape=pltpu.VMEM(mine.shape, mine.dtype),
        in_specs=[WHOLE] * 2,
        out_specs=WHOLE,
        compiler_params=params(2),
    )(mine, back)


def chosen_values(mine, back_keys, back):
    rows, width = mine.shape

    def kernel(mine_ref, back_keys_ref, back_ref, two_ref, one_ref, both_ref):
        choose(2, mine_ref, back_ref, two_ref)
        choose(3, mine_ref, back_ref, one_ref)
        both_ref[0:rows] = back_keys_ref[...]
        both_ref[rows:] = back_ref[...]

    one = pltpu.VMEM(mine.shape, mine.dtype)
    return pl.pallas_call(
        kernel,
        out_shape=(one, one, pltpu.VMEM((2 * rows, width), mine.dtype)),
        in_specs=[WHOLE] * 3,
        out_specs=(WHOLE,) * 3,
        compiler_params=params(2),
    )(mine, back_keys, back)


def estimate(rows, width, blocks, more=0):
    return pl.CostEstimate(
        flops=4 * rows * width * rows * blocks + more,
        bytes_accessed=2 * MIB,
        transcendentals=rows * (width // HEAD) * rows * blocks,
    )


def state_of(q):
    return [pltpu.VMEM(q.shape, F32)] * 3


def attend_part(q, first, pairs, distances, state, weight, half):
    arrays = [a for pair in pairs for a in pair]
    rows = pltpu.VMEM((weight.shape[0] // 2, weight.shape[1]), weight.dtype)
    return pl.pallas_call(
        functools.partial(part_kernel, distances, bool(state), half),
        out_shape=(*state_of(q), rows),
        in_specs=[WHOLE] * (2 + len(arrays) + len(state)) + [IN_HBM],
        out_specs=(WHOLE,) * 4,
        scratch_shapes=[pltpu.SemaphoreType.DMA((1,))],
        cost_estimate=estimate(*q.shape, len(pairs)),
        compiler_params=params(8),
    )(q, first, *arrays, *state, hbm(weight))


def flat(sources):
    stacked = tuple(not isinstance(s, tuple) for s in sources)
    return stacked, [a for s in sources for a in (s if isinstance(s, tuple) else (s,))]


def attend_last(q, first, sources, distances, state):
    stacked, arrays = flat(sources)
    return pl.pallas_call(
        functools.partial(last_kernel, distances, stacked),
        out_shape=pltpu.VMEM(q.shape, BF16),
        in_specs=[WHOLE] * (5 + len(arrays)),
        out_specs=WHOLE,
        cost_estimate=estimate(*q.shape, len(sources)),
        compiler_params=params(8),
    )(q, first, *arrays, *state)


def project_partner(att, weights):
    rows, half = att.shape[0], weights[0].shape[1] // 2
    return pl.pallas_call(
        partner_kernel,
        out_shape=pltpu.VMEM((rows, half), BF16),
        in_specs=[WHOLE] * 3,
        out_specs=WHOLE,
        cost_estimate=pl.CostEstimate(
            flops=2 * rows * att.shape[1] * half, bytes_accessed=2 * MIB, transcendentals=0
        ),
        compiler_params=params(4),
    )(att, *weights)


def project_kept(att, weights, residual):
    rows, half = residual.shape
    return pl.pallas_call(
        kept_kernel,
        out_shape=pltpu.VMEM((rows, half), F32),
        in_specs=[WHOLE] * 4,
        out_specs=WHOLE,
        cost_estimate=pl.CostEstimate(
            flops=2 * rows * att.shape[1] * half, bytes_accessed=2 * MIB, transcendentals=0
        ),
        compiler_params=params(4),
    )(att, *weights, residual)


def added(kept, received):
    return pl.pallas_call(
        add_kernel,
        out_shape=jax.ShapeDtypeStruct(received.shape, received.dtype),
        in_specs=[WHOLE] * 2,
        out_specs=IN_HBM,
        scratch_shapes=[
            pltpu.VMEM(received.shape, received.dtype),
            pltpu.SemaphoreType.DMA((4,)),
        ],
        compiler_params=params(4),
    )(kept, received)


def on_device(queries, keys, values, residual, out_weight):
    up = route("ctx", lambda i: i + 4)
    ring1 = route("ctx", lambda i: i // 4 * 4 + (i + 1) % 4)
    ring2 = route("ctx", lambda i: i // 4 * 4 + (i + 2) % 4)
    keys4 = lax.ppermute(keys, "ctx", up)
    values4 = lax.ppermute(values, "ctx", up)
    keys1 = lax.ppermute(keys, "ctx", route("ctx", lambda i: i + 1))
    q, k, v = staged(queries, keys, values)
    two = chosen_keys(k, keys4)
    keys2 = lax.ppermute(two, "ctx", ring2)
    two, one, both = chosen_values(v, keys4, values4)
    values2 = lax.ppermute(two, "ctx", ring2)
    back8 = lax.ppermute(both, "ctx", up)
    values1 = lax.ppermute(one, "ctx", ring1)
    *state, low = attend_part(
        q, k, [(k, v), (keys4, values4)], (0, 4), (), out_weight, 0
    )
    *state, high = attend_part(q, k, [(keys1, values1)], (1,), state, out_weight, 1)
    attended = attend_last(q, k, [(keys2, values2), back8], (2, 8), state)
    sent = project_partner(attended, (low, high))
    received = lax.ppermute(sent, "hid", [(0, 1), (1, 0)])
    kept = project_kept(attended, (low, high), residual)
    return added(kept, received)


def solution(mesh):
    return jax.shard_map(
        on_device,
        mesh=mesh,
        in_specs=(P("ctx", "hid"), P("ctx", "hid"), P("ctx", "hid"), P("ctx", "hid"), P("hid", None)),
        out_specs=P("ctx", "hid"),
        check_vma=False,
    )
```
